256 devices in a mesh: dp: 16 (over z_lo, x), tensor: 16 (over y, z_hi, core).
Axes of the slice: x: 4, y: 4, z: 8 (z_hi: 2, z_lo: 4; z = z_hi * 4 + z_lo), core: 2. Of those that a mesh axis runs over, the one named last changes fastest.
Arguments:
- out_grad: bfloat16 [2048, 5120], P('dp'), may hold values from -6 to 6
- gate_act: bfloat16 [2048, 25600], P('dp', 'tensor'), may hold values from -6 to 6
- up_act: bfloat16 [2048, 25600], P('dp', 'tensor'), may hold values from -6 to 6
- codes: int32 [5120, 25600], P('dp', 'tensor'), may hold values from 0 to 15
- zero_points: int32 [5120, 400], P('dp', 'tensor'), may hold values from 0 to 15
- scales: float32 [5120, 400], P('dp', 'tensor'), may hold values from 0.0009782797 to 0.003913119
- rotation: bfloat16 [1600, 1600], replicated, may hold values from -0.15625 to 0.15625
Outputs:
- grad_gate: bfloat16 [2048, 25600], P('dp', 'tensor')
- grad_up: bfloat16 [2048, 25600], P('dp', 'tensor')
- log_scale_grad: float32 [5120, 400], P('dp', 'tensor')
The draws below stay inside these ranges and needn't reach their ends.
All inputs are finite; a program needn't handle non-finite values.
Results may differ from the reference program's by a relative error of at most 0.011.
Values may be sent and summed in bfloat16 or wider, within the bound.
A program may use at most 128 MiB of HBM per device.

```python
import math
import jax
import jax.numpy as jnp
from jax import lax

D = 5120
FF = 25600
BLOCK = 1600
GROUP = 64
TOKENS = 2048
HAD = 16
GROUPS = 400


def plant(result, rng, least, largest):
    index_at = [jax.random.randint(jax.random.fold_in(rng, axis), (), 0, length) for axis, length in enumerate(result.shape)]
    widest = result.shape.index(max(result.shape))
    beside = index_at[:widest] + [(index_at[widest] + 1) % result.shape[widest]] + index_at[widest + 1:]
    return result.at[tuple(index_at)].set(least).at[tuple(beside)].set(largest)


def steps_of(stream_key, shape, split, low, top_value):
    gain = 1.0
    for axis_at, parts in split:
        heights = jax.random.uniform(jax.random.fold_in(jax.random.fold_in(stream_key, 6), axis_at), (parts,), jnp.float32, low / len(split), top_value / len(split))
        gain = gain * jnp.repeat(jnp.exp(heights), shape[axis_at] // parts).reshape((-1,) + (1,) * (len(shape) - 1 - axis_at))
    return gain


def scatter_about(stream_key, extent, scale, reach, pieces=(), kind=jnp.bfloat16):
    array = scale * jax.random.normal(stream_key, extent, jnp.float32)
    if pieces:
        array = array * steps_of(stream_key, extent, pieces, -0.22, 0.18)
    return jnp.clip(array, -reach, reach).astype(kind)


def setup_inputs(seed: int = 0) -> dict:
    key_of = jax.random.split(jax.random.key(seed), 8)
    return {
        "out_grad": scatter_about(key_of[0], (TOKENS, D), 1.0, 6.0, ((0, 16),)),
        "gate_act": scatter_about(key_of[1], (TOKENS, FF), 1.0, 6.0, ((0, 16), (1, 16))),
        "up_act": scatter_about(key_of[2], (TOKENS, FF), 1.0, 6.0, ((0, 16), (1, 16))),
        "codes": plant(jax.random.randint(key_of[3], (D, FF), 0, 16), jax.random.fold_in(key_of[3], 1), 0, 15).astype(jnp.int32),
        "zero_points": plant(jax.random.randint(key_of[4], (D, GROUPS), 0, 16), jax.random.fold_in(key_of[4], 1), 0, 15).astype(jnp.int32),
        "scales": jnp.clip(jnp.exp(math.log(0.003913119) - 1.3862944 * jax.random.uniform(key_of[5], (D, GROUPS), jnp.float32) ** steps_of(key_of[5], (D, GROUPS), ((0, 16), (1, 16)), -0.2, 0.2)), 0.0009782797, 0.003913119),
        "rotation": scatter_about(key_of[6], (BLOCK, BLOCK), BLOCK ** -0.5, 0.15625),
    }


def sylvester(order_size):
    indices = jnp.arange(order_size, dtype=jnp.int32)
    common_bits = indices[:, None] & indices[None, :]
    parity = jnp.zeros((order_size, order_size), jnp.int32)
    for bit_number in range(order_size.bit_length()):
        parity = parity + ((common_bits >> bit_number) & 1)
    return (1 - 2 * (parity % 2)).astype(jnp.float32)


def apply_hadamard(blocks):
    hadamard = sylvester(HAD)
    values = blocks.astype(jnp.float32).reshape(TOKENS, HAD, BLOCK)
    mixed = jnp.einsum("tab,ac->tcb", values, hadamard, precision=lax.Precision.HIGHEST)
    return (mixed * (1.0 / HAD ** 0.5)).astype(jnp.bfloat16).reshape(TOKENS, FF)


def reference(out_grad, gate_act, up_act, codes, zero_points, scales, rotation):
    gate32 = gate_act.astype(jnp.float32)
    up32 = up_act.astype(jnp.float32)
    sigmoid_gate = jax.nn.sigmoid(gate32)
    hidden = (gate32 * sigmoid_gate * up32).astype(jnp.bfloat16)
    mixed = jnp.dot(hidden.reshape(TOKENS * HAD, BLOCK), rotation, preferred_element_type=jnp.float32)
    mixed = mixed.astype(jnp.bfloat16).reshape(TOKENS, FF)
    rotated = apply_hadamard(mixed)
    levels = (codes.reshape(D, GROUPS, GROUP) - zero_points[:, :, None]).astype(jnp.float32)
    weight = (levels * scales[:, :, None]).astype(jnp.bfloat16).reshape(D, FF)
    grad_rotated = jnp.dot(out_grad, weight, preferred_element_type=jnp.float32).astype(jnp.bfloat16)
    grad_mixed = apply_hadamard(grad_rotated)
    grad_hidden = lax.dot_general(grad_mixed.reshape(TOKENS * HAD, BLOCK), rotation, (((1,), (1,)), ((), ())), preferred_element_type=jnp.float32)
    grad_hidden = grad_hidden.reshape(TOKENS, FF)
    grad_gate = (grad_hidden * up32 * sigmoid_gate * (1.0 + gate32 * (1.0 - sigmoid_gate))).astype(jnp.bfloat16)
    grad_up = (grad_hidden * gate32 * sigmoid_gate).astype(jnp.bfloat16)
    weight_grad = lax.dot_general(out_grad, rotated, (((0,), (0,)), ((), ())), preferred_element_type=jnp.float32)
    log_scale_grad = jnp.sum(weight_grad.reshape(D, GROUPS, GROUP) * levels, axis=2) * scales
    return grad_gate, grad_up, log_scale_grad
```

```python
import functools

import jax
import jax.numpy as jnp
from jax import lax
from jax.experimental import pallas as pl
from jax.experimental.pallas import tpu as pltpu
from jax.sharding import PartitionSpec as P

MESH = pl.DeviceIdType.MESH
F32 = jnp.float32
BF16 = jnp.bfloat16
TOK = 128
BLK = 1600
QR = 400
LO = 208
DROW = 320
DG = 1280
NC = 4
CR = BLK // NC
N_COPY = 110


def kernel(
    og_in, g_in, u_in, wmain, wrem, rot,
    o_gg, o_gu, o_ls,
    wfull, wrecv, og, m_buf, c_buf, yv, yo, h_buf, fp, fm, rott, pk,
    sp, sm, rp, rm, g_buf, a1, a2, s3, lsb, ssem, rsem,
):
    dp = lax.axis_index("dp")
    tn = lax.axis_index("tensor")
    x, zl = lax.rem(dp, 4), lax.div(dp, 4)
    y, zh, c = lax.div(tn, 4), lax.rem(lax.div(tn, 2), 2), lax.rem(tn, 2)
    pos = zh * 4 + zl

    def at_x(k):
        return (zl * 4 + lax.rem(x + 4 + k, 4), tn)

    def at_y(k):
        return (dp, lax.rem(y + 4 + k, 4) * 4 + zh * 2 + c)

    def at_z(k):
        to = lax.rem(pos + 8 + k, 8)
        return (lax.rem(to, 4) * 4 + x, y * 4 + lax.div(to, 4) * 2 + c)

    other = (dp, y * 4 + zh * 2 + 1 - c)

    count = [0]
    pending = []

    def send(src, dst, device):
        i = count[0]
        count[0] += 1
        copy = pltpu.make_async_remote_copy(
            src_ref=src, dst_ref=dst, send_sem=ssem.at[i], recv_sem=rsem.at[i],
            device_id=device, device_id_type=MESH,
        )
        copy.start()
        pending.append(copy)
        return copy

    barrier = pltpu.get_barrier_semaphore()
    peers = [at_x(1), at_x(2), at_x(3), at_y(1), at_y(2), at_y(3)]
    peers += [at_z(1), at_z(-1), at_z(2), at_z(-2), other]
    for peer in peers:
        pl.semaphore_signal(barrier, inc=1, device_id=peer, device_id_type=MESH)
    pl.semaphore_wait(barrier, len(peers))

    tile = lax.div(x, 2) * 5 + lax.rem(x, 2) * 3

    def main_at(j, q):
        xs = lax.rem(x + 4 + j, 4)
        at = pl.multiple_of((lax.div(xs, 2) * 5 + lax.rem(xs, 2) * 3) * 128, 128)
        return wfull.at[pl.ds(q * QR, QR), pl.ds(at, 256)]

    def rem_at(j, q):
        return wrecv.at[lax.rem(x + 4 + j, 4), q]

    w_plus, w_minus = [], []
    for q in range(4):
        own = wmain.at[pl.ds(q * QR, QR)]
        w_plus.append((send(own, main_at(0, q), at_x(1)), send(wrem.at[q], rem_at(0, q), at_x(1))))
        w_minus.append((send(own, main_at(0, q), at_x(-1)), send(wrem.at[q], rem_at(0, q), at_x(-1))))

    def og_cols(k):
        return pl.ds(pl.multiple_of(lax.rem(zl + 4 + k, 4) * DG, 128), DG)

    og_copies = [
        send(og_in.at[:, og_cols(1)], og.at[3], at_z(1)),
        send(og_in.at[:, og_cols(-1)], og.at[1], at_z(-1)),
        send(og_in.at[pl.ds(0, 64), og_cols(2)], og.at[2, pl.ds(0, 64)], at_z(2)),
        send(og_in.at[pl.ds(64, 64), og_cols(2)], og.at[2, pl.ds(64, 64)], at_z(-2)),
    ]

    def hidden_rows(i, _):
        rows = pl.ds(pl.multiple_of(i * 320, 16), 320)
        gate = g_in[rows, :].astype(F32)
        up = u_in[rows, :].astype(F32)
        sig = 1.0 / (1.0 + jnp.exp(-gate))
        gs = gate * sig
        m_buf[rows, :] = (gs * up).astype(BF16)
        a1[rows, :] = up * sig * (1.0 + gate * (1.0 - sig))
        a2[rows, :] = gs
        return 0

    lax.fori_loop(0, 5, hidden_rows, 0)
    hid = m_buf[...].astype(F32).T.astype(BF16)

    def mixed_cols(i, _):
        cols = pl.ds(pl.multiple_of(i * 256, 256), 256)
        part = jnp.dot(hid, rot[:, cols], preferred_element_type=F32)
        m_buf[pl.ds(pl.multiple_of(i * 256, 256), 256), :] = part.T.astype(BF16)
        return 0

    lax.fori_loop(0, 6, mixed_cols, 0)
    part = jnp.dot(hid, rot[:, 1536:1600], preferred_element_type=F32)
    m_buf[1536:1600, :] = part.T.astype(BF16)

    at_own = pl.multiple_of(tile * 128, 128)
    wfull[:, pl.ds(at_own, 256)] = wmain[...]
    wrecv[x] = wrem[...]
    og[0] = og_in[:, og_cols(0)]

    sign_c = jnp.where(c == 1, -1.0, 1.0).astype(F32)

    def over_core_and_y(src, slot, scale, dst):
        exchange = send(src, c_buf.at[slot], other)
        exchange.wait_recv()
        vals = yv.at[slot]
        outs = yo.at[slot]
        for q in range(4):
            rows = pl.ds(q * QR, QR)
            mine = src[rows, :].astype(F32) * sign_c + c_buf[slot, rows, :].astype(F32)
            outs[0, q] = mine.astype(BF16)
        copies = [
            send(outs.at[0, lax.rem(y + k, 4)], vals.at[y], at_y(k)) for k in (1, 3, 2)
        ]
        vals[y] = outs[0, y]
        for copy in copies:
            copy.wait_recv()
        v = [vals[i].astype(F32) for i in range(4)]
        p0, p1, n0, n1 = v[0] + v[1], v[2] + v[3], v[0] - v[1], v[2] - v[3]
        for i, value in enumerate((p0 + p1, n0 + n1, p0 - p1, n0 - n1)):
            outs[1, i] = (value * scale).astype(BF16)
        mine_at = pl.ds(pl.multiple_of(y * QR, 16), QR)
        copies = [
            send(outs.at[1, lax.rem(y + k, 4)], dst.at[mine_at], at_y(k)) for k in (1, 3, 2)
        ]
        dst[mine_at, :] = outs[1, y]
        return copies

    back = over_core_and_y(m_buf, 0, 1.0, h_buf)
    for copy in back:
        copy.wait_recv()

    def rows_of(n):
        return pl.ds(n * CR, CR)

    half_a, half_b = range(NC // 2), range(NC // 2, NC)
    got_p, got_m = {}, {}
    for n in range(NC):
        got_p[1, n] = send(h_buf.at[rows_of(n)], fp.at[0, rows_of(n)], at_z(1))
        got_m[1, n] = send(h_buf.at[rows_of(n)], fm.at[0, rows_of(n)], at_z(-1))

    w_two = []
    for q in (0, 1):
        for copy in w_plus[q]:
            copy.wait_recv()
        w_two.append((send(main_at(-1, q), main_at(-1, q), at_x(1)), send(rem_at(-1, q), rem_at(-1, q), at_x(1))))
    for q in (2, 3):
        for copy in w_minus[q]:
            copy.wait_recv()
        w_two.append((send(main_at(1, q), main_at(1, q), at_x(-1)), send(rem_at(1, q), rem_at(1, q), at_x(-1))))

    for k in (1, 2, 3):
        for n in range(NC):
            got_p[k, n].wait_recv()
            if k < 3 or n in half_a:
                got_p[k + 1, n] = send(fp.at[k - 1, rows_of(n)], fp.at[k, rows_of(n)], at_z(1))
            got_m[k, n].wait_recv()
            if k < 3 or n in half_b:
                got_m[k + 1, n] = send(fm.at[k - 1, rows_of(n)], fm.at[k, rows_of(n)], at_z(-1))

    for q in (2, 3):
        for copy in w_plus[q]:
            copy.wait_recv()
    for q in (0, 1):
        for copy in w_minus[q]:
            copy.wait_recv()
    for copies in w_two:
        for copy in copies:
            copy.wait_recv()
    for copy in og_copies:
        copy.wait_recv()
    low = lax.broadcasted_iota(jnp.int32, (LO, 128), 1) < 64
    for q in range(4):
        for pair in range(2):
            first = wrecv[2 * pair, q].astype(F32)
            second = wrecv[2 * pair + 1, q].astype(F32)
            lanes = pl.ds((pair * 5 + 2) * 128, 128)
            wfull[pl.ds(q * QR, LO), lanes] = jnp.where(low, first, second).astype(BF16)
            turned = pltpu.roll(jnp.where(low, second, first), 64, 1)
            wfull[pl.ds(q * QR + LO, QR - LO), lanes] = turned[: QR - LO].astype(BF16)
    og_all = og.reshape(4 * TOK, DG)
    for q in range(4):
        rows = pl.ds(q * QR, QR)
        part = lax.dot_general(
            wfull[rows, :], og_all[...], (((1,), (1,)), ((), ())), preferred_element_type=F32
        )
        for k in range(4):
            pk[k, rows, :] = part[:, k * TOK : (k + 1) * TOK]

    def sign_of(at):
        far = lax.div(lax.rem(pos + 8 + at, 8), 4)
        return jnp.where(far * zh == 1, -1.0, 1.0).astype(F32)

    sum_p, sum_m = {}, {}

    def send_p(d, n, add):
        value = pk[d % 4, rows_of(n), :] * sign_of(d)
        if add:
            sum_p[d, n].wait_recv()
            value = value + rp[d, rows_of(n), :].astype(F32)
        sp[d - 1, rows_of(n), :] = value.astype(BF16)
        sum_p[d - 1, n] = send(sp.at[d - 1, rows_of(n)], rp.at[d - 1, rows_of(n)], at_z(1))

    def send_m(d, n, add):
        value = pk[-d % 4, rows_of(n), :] * sign_of(-d)
        if add:
            sum_m[d, n].wait_recv()
            value = value + rm[d, rows_of(n), :].astype(F32)
        sm[d - 1, rows_of(n), :] = value.astype(BF16)
        sum_m[d - 1, n] = send(sm.at[d - 1, rows_of(n)], rm.at[d - 1, rows_of(n)], at_z(-1))

    for na, nb in zip(half_a, half_b):
        send_p(4, na, False)
        send_m(4, nb, False)
    for na, nb in zip(half_a, half_b):
        send_p(3, nb, False)
        send_m(3, na, False)

    for n in half_a:
        got_p[4, n].wait_recv()
    for n in half_b:
        got_m[4, n].wait_recv()

    def rotated(k):
        mine = h_buf if k == 0 else fm.at[k - 1]
        su, sv = sign_of(k) * 0.25, sign_of(k + 4) * 0.25
        lanes = pl.ds(k * TOK, TOK)
        for n in range(NC):
            if k == 0:
                far = fp if n in half_a else fm
                other_side = far[3, rows_of(n), :]
            else:
                other_side = fp[3 - k, rows_of(n), :]
            value = mine[rows_of(n), :].astype(F32) * su + other_side.astype(F32) * sv
            rott[rows_of(n), lanes] = value.astype(BF16)

    def weight_grad(i, _):
        rows = pl.ds(pl.multiple_of(i * 320, 16), 320)
        part = jnp.dot(rott[rows, :], og_all[...], preferred_element_type=F32)
        part = part * wfull[rows, :].astype(F32)
        s3[i, 0:5, :] = jnp.sum(part.reshape(5, 64, DG), axis=1)
        return 0

    for na, nb in zip(half_a, half_b):
        send_p(3, na, True)
        send_m(3, nb, True)
    for k in range(4):
        rotated(k)
    for na, nb in zip(half_a, half_b):
        send_p(2, nb, True)
        send_m(2, na, True)
    s3[...] = jnp.zeros_like(s3)
    lax.fori_loop(0, 3, weight_grad, 0)
    for na, nb in zip(half_a, half_b):
        send_p(2, na, True)
        send_m(2, nb, True)
    lax.fori_loop(3, 5, weight_grad, 0)

    def s_lanes(j):
        xs = lax.rem(x + 4 + j, 4)
        return pl.ds(pl.multiple_of((lax.div(xs, 2) * 5 + lax.rem(xs, 2) * 2) * 128, 128), 384)

    ls_copies = [
        send(s3.at[:, :, s_lanes(j)], lsb.at[j - 1], at_x(j)) for j in (1, 2, 3)
    ]
    for na, nb in zip(half_a, half_b):
        send_p(1, nb, True)
        send_m(1, na, True)
    for na, nb in zip(half_a, half_b):
        send_p(1, na, True)
        send_m(1, nb, True)
    for n in range(NC):
        sum_p[0, n].wait_recv()
        sum_m[0, n].wait_recv()
        value = pk[0, rows_of(n), :] * sign_of(0)
        value = value + rp[0, rows_of(n), :].astype(F32) + rm[0, rows_of(n), :].astype(F32)
        g_buf[0, rows_of(n), :] = value.astype(BF16)

    back = over_core_and_y(g_buf.at[0], 1, 0.25, g_buf.at[1])
    for copy in ls_copies:
        copy.wait_recv()
    total = s3[:, :, s_lanes(0)]
    for j in range(3):
        total = total + lsb[j]
    total = total.reshape(40, 384)
    turned = pltpu.roll(total, 320, 1)
    total = jnp.where(lax.rem(x, 2) == 1, turned, total)[:, :DROW]
    for i in range(5):
        rows = slice(5 * i, 5 * i + 5)
        o_ls[rows, :] = total[8 * i : 8 * i + 5, :]
    for copy in back:
        copy.wait_recv()

    def last_rows(i, _):
        rows = pl.ds(pl.multiple_of(i * 320, 16), 320)
        grad = jnp.dot(rot[rows, :], g_buf[1], preferred_element_type=F32)
        o_gg[rows, :] = (grad * a1[rows, :]).astype(BF16)
        o_gu[rows, :] = (grad * a2[rows, :]).astype(BF16)
        return 0

    lax.fori_loop(0, 5, last_rows, 0)
    for copy in pending:
        copy.wait_send()


def on_device(out_grad, gate_act, up_act, codes, zero_points, scales, rotation):
    levels = (codes.reshape(DROW, 25, 64) - zero_points[:, :, None]).astype(F32)
    weight = (levels * scales[:, :, None]).astype(BF16).reshape(DROW, BLK).T
    odd = lax.axis_index("dp") % 2 == 1
    wmain = jnp.where(odd, weight[:, 64:], weight[:, :256])
    rest = jnp.where(odd, weight[:, :64], weight[:, 256:]).reshape(4, QR, 64)
    first = rest[:, :LO]
    second = jnp.pad(rest[:, LO:], ((0, 0), (0, 2 * LO - QR), (0, 0)))
    wrem = jnp.where(
        odd, jnp.concatenate([second, first], 2), jnp.concatenate([first, second], 2)
    )
    vm = pl.BlockSpec(memory_space=pltpu.VMEM)
    gg, gu, ls = pl.pallas_call(
        kernel,
        out_shape=(
            jax.ShapeDtypeStruct((BLK, TOK), BF16),
            jax.ShapeDtypeStruct((BLK, TOK), BF16),
            jax.ShapeDtypeStruct((25, DROW), F32),
        ),
        in_specs=[vm] * 6,
        out_specs=(vm, vm, vm),
        scratch_shapes=[
            pltpu.VMEM((BLK, DG), BF16),
            pltpu.VMEM((4, 4, LO, 128), BF16),
            pltpu.VMEM((4, TOK, DG), BF16),
            pltpu.VMEM((BLK, TOK), BF16),
            pltpu.VMEM((2, BLK, TOK), BF16),
            pltpu.VMEM((2, 4, QR, TOK), BF16),
            pltpu.VMEM((2, 2, 4, QR, TOK), BF16),
            pltpu.VMEM((BLK, TOK), BF16),
            pltpu.VMEM((4, BLK, TOK), BF16),
            pltpu.VMEM((4, BLK, TOK), BF16),
            pltpu.VMEM((BLK, 4 * TOK), BF16),
            pltpu.VMEM((4, BLK, TOK), F32),
            pltpu.VMEM((4, BLK, TOK), BF16),
            pltpu.VMEM((4, BLK, TOK), BF16),
            pltpu.VMEM((4, BLK, TOK), BF16),
            pltpu.VMEM((4, BLK, TOK), BF16),
            pltpu.VMEM((2, BLK, TOK), BF16),
            pltpu.VMEM((BLK, TOK), F32),
            pltpu.VMEM((BLK, TOK), F32),
            pltpu.VMEM((5, 8, DG), F32),
            pltpu.VMEM((3, 5, 8, 384), F32),
            pltpu.SemaphoreType.DMA((N_COPY,)),
            pltpu.SemaphoreType.DMA((N_COPY,)),
        ],
        name="whole",
        compiler_params=pltpu.CompilerParams(
            collective_id=0, has_side_effects=True, vmem_limit_bytes=56 << 20
        ),
    )(out_grad, gate_act.T, up_act.T, wmain, wrem, rotation)
    return gg.T, gu.T, ls.T


def solution(mesh):
    return jax.shard_map(
        on_device,
        mesh=mesh,
        in_specs=(
            P("dp", None),
            P("dp", "tensor"),
            P("dp", "tensor"),
            P("dp", "tensor"),
            P("dp", "tensor"),
            P("dp", "tensor"),
            P(),
        ),
        out_specs=(P("dp", "tensor"), P("dp", "tensor"), P("dp", "tensor")),
        check_vma=False,
    )
```

```python
import jax
import jax.numpy as jnp
from jax import lax
from jax.experimental import pallas as pl
from jax.experimental.pallas import tpu as pltpu
from jax.sharding import PartitionSpec as P

MESH = pl.DeviceIdType.MESH
F32 = jnp.float32
BF16 = jnp.bfloat16
TOK = 128
BLK = 1600
DROW = 320
DG = 1280
REST = 832
HALF_A, HALF_B = (0, 2), (1, 3)
N_COPY = 154


def rows_of(n):
    return pl.ds(384 * n, size_of(n))


def size_of(n):
    return 384 if n < 3 else 448


def kernel(
    og_in, g_in, u_in, codes_in, zp_in, sc_in, rot_in,
    o_gg, o_gu, o_ls,
    codes, rot, g_v, u_v, wfull, wrecv, og, hid, m_buf, c_buf, mix, yv, yo, h_buf, fp, fm, rott, pk,
    sp, sm, rp, rm, g_buf, a1, a2, s3, lsb, zps, scs, lsem, ssem, rsem,
):
    dp = lax.axis_index("dp")
    tn = lax.axis_index("tensor")
    x, zl = lax.rem(dp, 4), lax.div(dp, 4)
    y, zh, c = lax.div(tn, 4), lax.rem(lax.div(tn, 2), 2), lax.rem(tn, 2)
    pos = zh * 4 + zl
    odd = lax.rem(x, 2)

    def at_x(k):
        return (zl * 4 + lax.rem(x + 4 + k, 4), tn)

    def at_y(k):
        return (dp, lax.rem(y + 4 + k, 4) * 4 + zh * 2 + c)

    def at_z(k):
        to = lax.rem(pos + 8 + k, 8)
        return (lax.rem(to, 4) * 4 + x, y * 4 + lax.div(to, 4) * 2 + c)

    other = (dp, y * 4 + zh * 2 + 1 - c)

    def og_cols(k):
        return pl.ds(pl.multiple_of(lax.rem(zl + 4 + k, 4) * DG, 128), DG)

    loads = [
        pltpu.make_async_copy(src, dst, lsem.at[i])
        for i, (src, dst) in enumerate(
            ((codes_in, codes), (g_in, g_v), (u_in, u_v), (rot_in, rot), (og_in.at[:, og_cols(0)], og.at[0]))
        )
    ]
    for load in loads:
        load.start()

    count = [0]
    pending = []

    def send(src, dst, device):
        i = count[0]
        count[0] += 1
        copy = pltpu.make_async_remote_copy(
            src_ref=src, dst_ref=dst, send_sem=ssem.at[i], recv_sem=rsem.at[i],
            device_id=device, device_id_type=MESH,
        )
        copy.start()
        pending.append(copy)
        return copy

    barrier = pltpu.get_barrier_semaphore()
    peers = [at_x(1), at_x(2), at_x(3), at_y(1), at_y(2), at_y(3)]
    peers += [at_z(1), at_z(-1), at_z(2), at_z(-2), other]
    for peer in peers:
        pl.semaphore_signal(barrier, inc=1, device_id=peer, device_id_type=MESH)
    pl.semaphore_wait(barrier, len(peers))

    half = pl.ds(pl.multiple_of(c * 64, 64), 64)
    first, second = (pl.ds(pl.multiple_of(c * 64 + i * 32, 32), 32) for i in (0, 1))
    og_far = [
        (send(og_in.at[half, og_cols(1)], og.at[3, half], at_z(1)),),
        (send(og_in.at[half, og_cols(-1)], og.at[1, half], at_z(-1)),),
        (
            send(og_in.at[first, og_cols(2)], og.at[2, first], at_z(2)),
            send(og_in.at[second, og_cols(2)], og.at[2, second], at_z(-2)),
        ),
    ]

    def lanes_of(j):
        xs = lax.rem(x + 4 + j, 4)
        return pl.ds(pl.multiple_of((lax.div(xs, 2) * 5 + lax.rem(xs, 2) * 3) * 128, 128), 256)

    def main_part(j, n, part, parts):
        size = size_of(n) // parts
        return wfull.at[pl.ds(384 * n + part * size, size), lanes_of(j)]

    def rest_part(j, n, part, parts):
        size = (192 if n < 3 else 256) // parts
        return wrecv.at[lax.rem(x + 4 + j, 4), pl.ds(192 * n + part * size, size)]

    def place(src, dst):
        dst[0:25, 0:DROW] = src[...].astype(F32)
        value = dst[:, 0:384]
        main = jnp.where(odd == 1, pltpu.roll(value, 320, 1), value)[:, :256]
        rest = jnp.where(odd == 1, value[:, :128], value[:, 256:])
        dst[:, 0:256] = main
        dst[:, 256:384] = rest
        dst[:, 384:512] = pltpu.roll(rest, 64, 1)

    def rest_of(src, g):
        here, after = src[pl.ds(g, 1), :], src[pl.ds(g + 1, 1), :]
        left, right = jnp.where(odd == 1, after, here), jnp.where(odd == 1, here, after)
        return jnp.where(low[:1], left[:, 256:384], right[:, 384:512])

    low = lax.broadcasted_iota(jnp.int32, (64, 128), 1) < 64
    main_rows = pl.ds(pl.multiple_of(odd * 64, 64), 256)
    rest_rows = pl.ds(pl.multiple_of(256 - odd * 256, 64), 64)

    def weight_tile(i, width):
        at = pl.ds(i * 128, width) if isinstance(i, int) else pl.ds(pl.multiple_of(i * 128, 128), width)
        main = codes[main_rows, at].astype(F32).T
        rest = codes[rest_rows, at].astype(F32)
        if width == 128:
            turned = pltpu.roll(rest, 64, 1)
            stack = jnp.where(odd == 1, jnp.concatenate([turned, rest]), jnp.concatenate([rest, turned]))
            packed = stack.T[:64]
        else:
            packed = jnp.concatenate([rest, rest]).T
        for k in range(width // 64):
            g = 2 * i + k
            value = (main[64 * k : 64 * k + 64] - zps[pl.ds(g, 1), 0:256]) * scs[pl.ds(g, 1), 0:256]
            wfull[pl.ds(i * 128 + 64 * k if isinstance(i, int) else pl.multiple_of(i * 128 + 64 * k, 64), 64), lanes_of(0)] = value.astype(BF16)
        if width == 128:
            zp, sc = rest_of(zps, 2 * i), rest_of(scs, 2 * i)
        else:
            zp, sc = (jnp.where(low[:1], a[24:25, 256:384], a[24:25, 384:512]) for a in (zps, scs))
        wrecv[x, pl.ds(i * 64 if isinstance(i, int) else pl.multiple_of(i * 64, 64), 64), :] = ((packed - zp) * sc).astype(BF16)

    w_plus, w_minus, w_two = {}, {}, {}

    def weights(n):
        def step(i, _):
            weight_tile(3 * n + i, 128)
            return 0

        lax.fori_loop(0, 3, step, 0)
        if n == 3:
            weight_tile(12, 64)
        for kept, k in ((w_plus, 1), (w_minus, -1)):
            kept[n] = [send(part(0, n, 0, 1), part(0, n, 0, 1), at_x(k)) for part in (main_part, rest_part)]

    def weights_on(n):
        for copy in w_plus[n]:
            copy.wait_recv()
        w_two[n] = [send(part(-1, n, 0, 2), part(-1, n, 0, 2), at_x(1)) for part in (main_part, rest_part)]
        for copy in w_minus[n]:
            copy.wait_recv()
        w_two[n] += [send(part(1, n, 1, 2), part(1, n, 1, 2), at_x(-1)) for part in (main_part, rest_part)]

    def unpack(n):
        for i in range(3 * n, 3 * n + (3 if n < 3 else 4)):
            for pair in range(2):
                even = wrecv[2 * pair, pl.ds(64 * i, 64), :].astype(F32)
                next_ = wrecv[2 * pair + 1, pl.ds(64 * i, 64), :].astype(F32)
                lanes = pl.ds((pair * 5 + 2) * 128, 128)
                wfull[pl.ds(128 * i, 64), lanes] = jnp.where(low, even, next_).astype(BF16)
                if i < 12:
                    turned = pltpu.roll(jnp.where(low, next_, even), 64, 1)
                    wfull[pl.ds(128 * i + 64, 64), lanes] = turned.astype(BF16)

    def hidden_rows(i, _):
        rows = pl.ds(pl.multiple_of(i * 320, 16), 320)
        gate = g_v[rows, :].astype(F32)
        up = u_v[rows, :].astype(F32)
        sig = 1.0 / (1.0 + jnp.exp(-gate))
        gs = gate * sig
        m_buf[rows, :] = (gs * up).astype(BF16)
        a1[rows, :] = up * sig * (1.0 + gate * (1.0 - sig))
        a2[rows, :] = gs
        return 0

    def mixed(n):
        part = jnp.dot(hid[...], rot[:, 384 * n : 384 * n + size_of(n)], preferred_element_type=F32)
        mix[0, rows_of(n), :] = part.T.astype(BF16)

    sign_c = jnp.where(c == 1, -1.0, 1.0).astype(F32)
    over_core, over_y, over_back = {}, {}, {}
    dst_of = (h_buf, g_buf)

    def part_at(n, i):
        size = size_of(n) // 4
        return pl.ds(pl.multiple_of(384 * n + i * size, 16), size)

    def had1(slot, n):
        over_core[slot, n] = send(mix.at[slot, rows_of(n)], c_buf.at[slot, rows_of(n)], other)

    def had2(slot, n):
        over_core[slot, n].wait_recv()
        rows, few = rows_of(n), pl.ds(96 * n, size_of(n) // 4)
        mine = mix[slot, rows, :].astype(F32) * sign_c + c_buf[slot, rows, :].astype(F32)
        m2 = mix.at[2 + slot]
        m2[rows, :] = mine.astype(BF16)
        over_y[slot, n] = [
            send(m2.at[part_at(n, lax.rem(y + k, 4))], yv.at[slot, y, few], at_y(k)) for k in (2, 1, 3)
        ]
        yv[slot, y, few, :] = m2[part_at(n, y), :]

    def had3(slot, n):
        for copy in over_y[slot, n]:
            copy.wait_recv()
        few = pl.ds(96 * n, size_of(n) // 4)
        v = [yv[slot, i, few, :].astype(F32) for i in range(4)]
        p0, p1, n0, n1 = v[0] + v[1], v[2] + v[3], v[0] - v[1], v[2] - v[3]
        scale = 0.25 if slot else 1.0
        for i, value in enumerate((p0 + p1, n0 + n1, p0 - p1, n0 - n1)):
            yo[slot, i, few, :] = (value * scale).astype(BF16)
        dst = dst_of[slot]
        over_back[slot, n] = [
            send(yo.at[slot, lax.rem(y + k, 4), few], dst.at[part_at(n, y)], at_y(k)) for k in (2, 1, 3)
        ]
        dst[part_at(n, y), :] = yo[slot, y, few, :]

    def had4(slot, n):
        for copy in over_back[slot, n]:
            copy.wait_recv()

    got_p, got_m = {}, {}

    def ag(k, n):
        rows = rows_of(n)
        if k == 1:
            had4(0, n)
            got_p[1, n] = send(h_buf.at[rows], fp.at[0, rows], at_z(1))
            got_m[1, n] = send(h_buf.at[rows], fm.at[0, rows], at_z(-1))
            return
        got_p[k - 1, n].wait_recv()
        if k < 4 or n in HALF_A:
            got_p[k, n] = send(fp.at[k - 2, rows], fp.at[k - 1, rows], at_z(1))
        got_m[k - 1, n].wait_recv()
        if k < 4 or n in HALF_B:
            got_m[k, n] = send(fm.at[k - 2, rows], fm.at[k - 1, rows], at_z(-1))

    og_all = og.reshape(4 * TOK, DG)

    def grad_part(n):
        for copy in w_two[n]:
            copy.wait_recv()
        unpack(n)
        rows = rows_of(n)
        part = lax.dot_general(
            wfull[rows, :], og_all[...], (((1,), (1,)), ((), ())), preferred_element_type=F32
        )
        for k in range(4):
            pk[k, rows, :] = part[:, k * TOK : (k + 1) * TOK]

    def sign_of(at):
        far = lax.div(lax.rem(pos + 8 + at, 8), 4)
        return jnp.where(far * zh == 1, -1.0, 1.0).astype(F32)

    sum_p, sum_m = {}, {}

    def send_sum(up, d, n):
        rows = rows_of(n)
        kept, got, out, way = (sum_p, rp, sp, 1) if up else (sum_m, rm, sm, -1)
        value = pk[way * d % 4, rows, :] * sign_of(way * d)
        if (d, n) in kept:
            kept[d, n].wait_recv()
            value = value + got[d, rows, :].astype(F32)
        out[d - 1, rows, :] = value.astype(BF16)
        kept[d - 1, n] = send(out.at[d - 1, rows], got.at[d - 1, rows], at_z(way))

    def rs(step, n):
        long_up = n in HALF_A
        for up in (long_up, not long_up):
            d = (4 if up == long_up else 3) - step
            if d >= 1:
                send_sum(up, d, n)

    def rs_end(n):
        rows = rows_of(n)
        sum_p[0, n].wait_recv()
        sum_m[0, n].wait_recv()
        value = pk[0, rows, :] * sign_of(0)
        value = value + rp[0, rows, :].astype(F32) + rm[0, rows, :].astype(F32)
        mix[1, rows, :] = value.astype(BF16)
        had1(1, n)

    def rotated(n):
        rows = rows_of(n)
        (got_p if n in HALF_A else got_m)[4, n].wait_recv()
        for k in range(4):
            mine = h_buf if k == 0 else fm.at[k - 1]
            far = fp.at[3 - k] if k else (fp if n in HALF_A else fm).at[3]
            value = mine[rows, :].astype(F32) * (sign_of(k) * 0.25)
            value = value + far[rows, :].astype(F32) * (sign_of(k + 4) * 0.25)
            rott[rows, pl.ds(k * TOK, TOK)] = value.astype(BF16)

    def weight_grad(n):
        rows, groups = rows_of(n), size_of(n) // 64
        part = jnp.dot(rott[rows, :], og_all[...], preferred_element_type=F32)
        part = part * wfull[rows, :].astype(F32)
        s3[n, 0:groups, :] = jnp.sum(part.reshape(groups, 64, DG), axis=1)

    def s_lanes(j):
        xs = lax.rem(x + 4 + j, 4)
        return pl.ds(pl.multiple_of((lax.div(xs, 2) * 5 + lax.rem(xs, 2) * 2) * 128, 128), 384)

    place(zp_in, zps)
    place(sc_in, scs)
    loads[0].wait()
    weights(0)
    loads[1].wait()
    loads[2].wait()
    lax.fori_loop(0, 5, hidden_rows, 0)
    hid[...] = m_buf[...].astype(F32).T.astype(BF16)
    loads[3].wait()
    mixed(0)
    had1(0, 0)
    weights(1)
    mixed(1)
    had1(0, 1)
    had2(0, 0)
    mixed(2)
    had1(0, 2)
    had2(0, 1)
    had3(0, 0)
    weights(2)
    mixed(3)
    had1(0, 3)
    had2(0, 2)
    had3(0, 1)
    weights_on(0)
    weights(3)
    ag(1, 0)
    had2(0, 3)
    had3(0, 2)
    ag(1, 1)
    og_near = []
    for k, copies in zip((3, 1, 2), og_far):
        for copy in copies:
            copy.wait_recv()
        og_near.append(send(og.at[k, half], og.at[k, half], other))
    had3(0, 3)
    ag(1, 2)
    weights_on(1)
    ag(1, 3)
    loads[4].wait()
    for copy in og_near:
        copy.wait_recv()
    s3[...] = jnp.zeros_like(s3)
    grad_part(0)
    rs(0, 0)
    ag(2, 0)
    ag(2, 1)
    weights_on(2)
    rs(1, 0)
    grad_part(1)
    rs(0, 1)
    ag(2, 2)
    rs(2, 0)
    ag(2, 3)
    rs(1, 1)
    weights_on(3)
    grad_part(2)
    rs(0, 2)
    rs(3, 0)
    ag(3, 0)
    rs(2, 1)
    rs(1, 2)
    ag(3, 1)
    rs_end(0)
    grad_part(3)
    rs(0, 3)
    rs(3, 1)
    had2(1, 0)
    rs(2, 2)
    ag(3, 2)
    rs(1, 3)
    had3(1, 0)
    rs_end(1)
    rs(3, 2)
    ag(3, 3)
    had2(1, 1)
    rs(2, 3)
    ag(4, 0)
    rs_end(2)
    had3(1, 1)
    rs(3, 3)
    ag(4, 1)
    had2(1, 2)
    ag(4, 2)
    ag(4, 3)
    had3(1, 2)
    rotated(0)
    weight_grad(0)
    rs_end(3)
    rotated(1)
    weight_grad(1)
    had2(1, 3)
    rotated(2)
    weight_grad(2)
    had3(1, 3)
    rotated(3)
    weight_grad(3)
    ls_copies = [
        send(s3.at[:, :, s_lanes(j)], lsb.at[j - 1], at_x(j)) for j in (1, 2, 3)
    ]
    for n in range(4):
        had4(1, n)

    def last_rows(i, _):
        rows = pl.ds(pl.multiple_of(i * 320, 16), 320)
        grad = jnp.dot(rot[rows, :], g_buf[...], preferred_element_type=F32)
        o_gg[rows, :] = (grad * a1[rows, :]).astype(BF16)
        o_gu[rows, :] = (grad * a2[rows, :]).astype(BF16)
        return 0

    lax.fori_loop(0, 5, last_rows, 0)
    for copy in ls_copies:
        copy.wait_recv()
    total = s3[:, :, s_lanes(0)]
    for j in range(3):
        total = total + lsb[j]
    total = total.reshape(32, 384)
    total = jnp.where(odd == 1, pltpu.roll(total, 320, 1), total)[:, :DROW]
    for n in range(4):
        groups = size_of(n) // 64
        o_ls[6 * n : 6 * n + groups, :] = total[8 * n : 8 * n + groups, :]
    for copy in pending:
        copy.wait_send()


def on_device(out_grad, gate_act, up_act, codes, zero_points, scales, rotation):
    vm = pl.BlockSpec(memory_space=pltpu.VMEM)
    hbm = pl.BlockSpec(memory_space=pl.ANY)
    gg, gu, ls = pl.pallas_call(
        kernel,
        out_shape=(
            jax.ShapeDtypeStruct((BLK, TOK), BF16),
            jax.ShapeDtypeStruct((BLK, TOK), BF16),
            jax.ShapeDtypeStruct((25, DROW), F32),
        ),
        in_specs=[hbm, hbm, hbm, hbm, vm, vm, hbm],
        out_specs=(vm, vm, vm),
        scratch_shapes=[
            pltpu.VMEM((DROW, BLK), jnp.int32),
            pltpu.VMEM((BLK, BLK), BF16),
            pltpu.VMEM((BLK, TOK), BF16),
            pltpu.VMEM((BLK, TOK), BF16),
            pltpu.VMEM((BLK, DG), BF16),
            pltpu.VMEM((4, REST, 128), BF16),
            pltpu.VMEM((4, TOK, DG), BF16),
            pltpu.VMEM((TOK, BLK), BF16),
            pltpu.VMEM((BLK, TOK), BF16),
            pltpu.VMEM((2, BLK, TOK), BF16),
            pltpu.VMEM((4, BLK, TOK), BF16),
            pltpu.VMEM((2, 4, BLK // 4, TOK), BF16),
            pltpu.VMEM((2, 4, BLK // 4, TOK), BF16),
            pltpu.VMEM((BLK, TOK), BF16),
            pltpu.VMEM((4, BLK, TOK), BF16),
            pltpu.VMEM((4, BLK, TOK), BF16),
            pltpu.VMEM((BLK, 4 * TOK), BF16),
            pltpu.VMEM((4, BLK, TOK), F32),
            pltpu.VMEM((4, BLK, TOK), BF16),
            pltpu.VMEM((4, BLK, TOK), BF16),
            pltpu.VMEM((4, BLK, TOK), BF16),
            pltpu.VMEM((4, BLK, TOK), BF16),
            pltpu.VMEM((BLK, TOK), BF16),
            pltpu.VMEM((BLK, TOK), F32),
            pltpu.VMEM((BLK, TOK), F32),
            pltpu.VMEM((4, 8, DG), F32),
            pltpu.VMEM((3, 4, 8, 384), F32),
            pltpu.VMEM((32, 512), F32),
            pltpu.VMEM((32, 512), F32),
            pltpu.SemaphoreType.DMA((5,)),
            pltpu.SemaphoreType.DMA((N_COPY,)),
            pltpu.SemaphoreType.DMA((N_COPY,)),
        ],
        name="whole",
        compiler_params=pltpu.CompilerParams(
            collective_id=0, has_side_effects=True, vmem_limit_bytes=56 << 20
        ),
    )(out_grad, gate_act.T, up_act.T, codes, zero_points.T, scales.T, rotation)
    return gg.T, gu.T, ls.T


def solution(mesh):
    return jax.shard_map(
        on_device,
        mesh=mesh,
        in_specs=(
            P("dp", None),
            P("dp", "tensor"),
            P("dp", "tensor"),
            P("dp", "tensor"),
            P("dp", "tensor"),
            P("dp", "tensor"),
            P(),
        ),
        out_specs=(P("dp", "tensor"), P("dp", "tensor"), P("dp", "tensor")),
        check_vma=False,
    )
```

```python
import jax
import jax.numpy as jnp
from jax import lax
from jax.experimental import pallas as pl
from jax.experimental.pallas import tpu as pltpu
from jax.sharding import PartitionSpec as P

MESH = pl.DeviceIdType.MESH
F32 = jnp.float32
BF16 = jnp.bfloat16
TOK = 128
BLK = 1600
DROW = 320
DG = 1280
REST = 832
HALF_A, HALF_B = (0, 2), (1, 3)
N_COPY = 178


ORDER = (
    ("hidden",), ("mixed", 0), ("mixed", 1), ("weights", 0), ("had3", 0, 0), ("mixed", 2), ("mixed", 3),
    ("had3", 0, 1), ("weights", 1), ("ag", 1, 0), ("had3", 0, 2), ("weights_on", 0), ("weights", 2), ("had3", 0, 3),
    ("ag", 2, 0), ("ag", 1, 1), ("og_on",), ("ag", 1, 2), ("weights_on", 1), ("weights", 3), ("ag", 1, 3),
    ("grad_part", 0), ("rs", 0, 0), ("ag", 2, 1), ("ag", 2, 2), ("weights_on", 2), ("rs", 1, 0), ("grad_part", 1),
    ("rs", 0, 1), ("ag", 3, 1), ("rs", 2, 0), ("rs", 1, 1), ("weights_on", 3), ("ag", 4, 1), ("grad_part", 2),
    ("rs", 0, 2), ("rs", 3, 0), ("rs", 2, 1), ("grad_part", 3), ("rs", 0, 3), ("rotated", 1), ("weight_grad", 1),
    ("rs", 1, 2), ("rs_end", 0), ("rs", 3, 1), ("ag", 2, 3), ("rs", 1, 3), ("had3", 1, 0), ("rs", 2, 2),
    ("rs_end", 1), ("last_part", 0), ("ag", 3, 2), ("rs", 2, 3), ("had3", 1, 1), ("rs", 3, 2), ("ag", 3, 3),
    ("last_part", 1), ("ag", 3, 0), ("rs", 3, 3), ("rs_end", 2), ("ag", 4, 2), ("ag", 4, 3), ("ag", 4, 0),
    ("had3", 1, 2), ("rs_end", 3), ("rotated", 2), ("weight_grad", 2), ("rotated", 3), ("weight_grad", 3),
    ("rotated", 0), ("weight_grad", 0), ("ls_send",), ("had3", 1, 3), ("last_part", 2), ("ls_end",), ("last_part", 3),
)

def rows_of(n):
    return pl.ds(384 * n, size_of(n))


def size_of(n):
    return 384 if n < 3 else 448


def kernel(
    og_in, g_in, u_in, codes_in, zp_in, sc_in, rot_in,
    o_gh, o_ls,
    codes, rot, g_v, u_v, wfull, wrecv, og, hid, m_buf, mix, yv, yo, h_buf, fp, fm, rott, pk,
    sp, sm, rp, rm, g_buf, s3, lsb, z_v, s_v, zps, scs, lsem, ssem, rsem,
):
    dp = lax.axis_index("dp")
    tn = lax.axis_index("tensor")
    x, zl = lax.rem(dp, 4), lax.div(dp, 4)
    y, zh, c = lax.div(tn, 4), lax.rem(lax.div(tn, 2), 2), lax.rem(tn, 2)
    pos = zh * 4 + zl
    odd = lax.rem(x, 2)

    def at_x(k):
        return (zl * 4 + lax.rem(x + 4 + k, 4), tn)

    def at_y(k):
        return (dp, lax.rem(y + 4 + k, 4) * 4 + zh * 2 + c)

    def across(k):
        return (dp, lax.rem(y + 4 + k, 4) * 4 + zh * 2 + 1 - c)

    def at_z(k):
        to = lax.rem(pos + 8 + k, 8)
        return (lax.rem(to, 4) * 4 + x, y * 4 + lax.div(to, 4) * 2 + c)

    other = across(0)

    def og_cols(k):
        return pl.ds(pl.multiple_of(lax.rem(zl + 4 + k, 4) * DG, 128), DG)

    moves = {"gate": (g_in, g_v), "up": (u_in, u_v), "zp": (zp_in, z_v), "sc": (sc_in, s_v)}
    for n in range(4):
        cols = rows_of(n)
        moves["rot", n] = (rot_in.at[:, cols], rot.at[:, cols])
        moves["codes", n] = (codes_in.at[:, cols], codes.at[:, cols])
    moves["og"] = (og_in.at[:, og_cols(0)], og.at[0])
    loads = {
        name: pltpu.make_async_copy(src, dst, lsem.at[i])
        for i, (name, (src, dst)) in enumerate(moves.items())
    }
    def load(*names):
        for name in names:
            loads[name].start()

    load("gate", "up", ("rot", 0))

    count = [0]
    pending = []

    def send(src, dst, device):
        i = count[0]
        count[0] += 1
        copy = pltpu.make_async_remote_copy(
            src_ref=src, dst_ref=dst, send_sem=ssem.at[i], recv_sem=rsem.at[i],
            device_id=device, device_id_type=MESH,
        )
        copy.start()
        pending.append(copy)
        return copy

    barrier = pltpu.get_barrier_semaphore()
    peers = [at_x(1), at_x(2), at_x(3), at_y(1), at_y(2), at_y(3)]
    peers += [at_z(1), at_z(-1), at_z(2), at_z(-2), other, across(1), across(2), across(3)]
    for peer in peers:
        pl.semaphore_signal(barrier, inc=1, device_id=peer, device_id_type=MESH)
    pl.semaphore_wait(barrier, len(peers))

    half = pl.ds(pl.multiple_of(c * 64, 64), 64)
    first, second = (pl.ds(pl.multiple_of(c * 64 + i * 32, 32), 32) for i in (0, 1))
    og_far = []

    def og_start():
        og_far.append((send(og_in.at[half, og_cols(1)], og.at[3, half], at_z(1)),))
        og_far.append((send(og_in.at[half, og_cols(-1)], og.at[1, half], at_z(-1)),))
        og_far.append((
            send(og_in.at[first, og_cols(2)], og.at[2, first], at_z(2)),
            send(og_in.at[second, og_cols(2)], og.at[2, second], at_z(-2)),
        ))

    def lanes_of(j):
        xs = lax.rem(x + 4 + j, 4)
        return pl.ds(pl.multiple_of((lax.div(xs, 2) * 5 + lax.rem(xs, 2) * 3) * 128, 128), 256)

    def main_part(j, n, part, parts):
        size = size_of(n) // parts
        return wfull.at[pl.ds(384 * n + part * size, size), lanes_of(j)]

    def rest_part(j, n, part, parts):
        size = (192 if n < 3 else 256) // parts
        return wrecv.at[lax.rem(x + 4 + j, 4), pl.ds(192 * n + part * size, size)]

    def place(src, dst):
        dst[0:25, 0:DROW] = src[...].astype(F32)
        value = dst[:, 0:384]
        main = jnp.where(odd == 1, pltpu.roll(value, 320, 1), value)[:, :256]
        rest = jnp.where(odd == 1, value[:, :128], value[:, 256:])
        dst[:, 0:256] = main
        dst[:, 256:384] = rest
        dst[:, 384:512] = pltpu.roll(rest, 64, 1)

    def rest_of(src, g):
        here, after = src[pl.ds(g, 1), :], src[pl.ds(g + 1, 1), :]
        left, right = jnp.where(odd == 1, after, here), jnp.where(odd == 1, here, after)
        return jnp.where(low[:1], left[:, 256:384], right[:, 384:512])

    low = lax.broadcasted_iota(jnp.int32, (64, 128), 1) < 64
    main_rows = pl.ds(pl.multiple_of(odd * 64, 64), 256)
    rest_rows = pl.ds(pl.multiple_of(256 - odd * 256, 64), 64)

    def weight_tile(i, width):
        at = pl.ds(i * 128, width) if isinstance(i, int) else pl.ds(pl.multiple_of(i * 128, 128), width)
        main = codes[main_rows, at].astype(F32).T
        rest = codes[rest_rows, at].astype(F32)
        if width == 128:
            turned = pltpu.roll(rest, 64, 1)
            stack = jnp.where(odd == 1, jnp.concatenate([turned, rest]), jnp.concatenate([rest, turned]))
            packed = stack.T[:64]
        else:
            packed = jnp.concatenate([rest, rest]).T
        for k in range(width // 64):
            g = 2 * i + k
            value = (main[64 * k : 64 * k + 64] - zps[pl.ds(g, 1), 0:256]) * scs[pl.ds(g, 1), 0:256]
            wfull[pl.ds(i * 128 + 64 * k if isinstance(i, int) else pl.multiple_of(i * 128 + 64 * k, 64), 64), lanes_of(0)] = value.astype(BF16)
        if width == 128:
            zp, sc = rest_of(zps, 2 * i), rest_of(scs, 2 * i)
        else:
            zp, sc = (jnp.where(low[:1], a[24:25, 256:384], a[24:25, 384:512]) for a in (zps, scs))
        wrecv[x, pl.ds(i * 64 if isinstance(i, int) else pl.multiple_of(i * 64, 64), 64), :] = ((packed - zp) * sc).astype(BF16)

    w_plus, w_minus, w_two = {}, {}, {}

    def weights(n):
        def step(i, _):
            weight_tile(3 * n + i, 128)
            return 0

        if n == 0:
            loads["zp"].wait()
            loads["sc"].wait()
            place(z_v, zps)
            place(s_v, scs)
        loads["codes", n].wait()
        lax.fori_loop(0, 3, step, 0)
        if n == 3:
            weight_tile(12, 64)
        for kept, k in ((w_plus, 1), (w_minus, -1)):
            kept[n] = [send(part(0, n, 0, 1), part(0, n, 0, 1), at_x(k)) for part in (main_part, rest_part)]

    def weights_on(n):
        for copy in w_plus[n]:
            copy.wait_recv()
        w_two[n] = [send(part(-1, n, 0, 2), part(-1, n, 0, 2), at_x(1)) for part in (main_part, rest_part)]
        for copy in w_minus[n]:
            copy.wait_recv()
        w_two[n] += [send(part(1, n, 1, 2), part(1, n, 1, 2), at_x(-1)) for part in (main_part, rest_part)]

    def unpack(n):
        for i in range(3 * n, 3 * n + (3 if n < 3 else 4)):
            for pair in range(2):
                even = wrecv[2 * pair, pl.ds(64 * i, 64), :].astype(F32)
                next_ = wrecv[2 * pair + 1, pl.ds(64 * i, 64), :].astype(F32)
                lanes = pl.ds((pair * 5 + 2) * 128, 128)
                wfull[pl.ds(128 * i, 64), lanes] = jnp.where(low, even, next_).astype(BF16)
                if i < 12:
                    turned = pltpu.roll(jnp.where(low, next_, even), 64, 1)
                    wfull[pl.ds(128 * i + 64, 64), lanes] = turned.astype(BF16)

    def hidden_rows(i, _):
        rows = pl.ds(pl.multiple_of(i * 320, 16), 320)
        gate = g_v[rows, :].astype(F32)
        up = u_v[rows, :].astype(F32)
        m_buf[rows, :] = (gate * (1.0 / (1.0 + jnp.exp(-gate))) * up).astype(BF16)
        return 0

    def hidden():
        loads["gate"].wait()
        loads["up"].wait()
        lax.fori_loop(0, 5, hidden_rows, 0)
        hid[...] = m_buf[...].astype(F32).T.astype(BF16)
        load(("codes", 0), "zp", "sc", ("rot", 1))

    def mixed(n):
        loads["rot", n].wait()
        part = jnp.dot(hid[...], rot[:, 384 * n : 384 * n + size_of(n)], preferred_element_type=F32)
        mix[0, rows_of(n), :] = part.T.astype(BF16)
        had2(0, n)
        if n == 0:
            load(("rot", 2), ("rot", 3))
            og_start()
        elif n == 1:
            load(("codes", 1), ("codes", 2), ("codes", 3), "og")

    sign_c = jnp.where(c == 1, -1.0, 1.0).astype(F32)
    over_y, over_back = {}, {}
    dst_of = (h_buf, g_buf)

    def part_at(n, i):
        size = size_of(n) // 4
        return pl.ds(pl.multiple_of(384 * n + i * size, 16), size)

    def had2(slot, n):
        src, few = mix.at[slot], pl.ds(96 * n, size_of(n) // 4)
        over_y[slot, n] = [
            send(src.at[part_at(n, lax.rem(y + k, 4))], yv.at[slot, 4 * c + y, few], to(k))
            for to, k in ((across, 2), (at_y, 2), (across, 1), (at_y, 1), (across, 3), (at_y, 3), (across, 0))
        ]
        yv[slot, 4 * c + y, few, :] = src[part_at(n, y), :]

    def had3(slot, n):
        for copy in over_y[slot, n]:
            copy.wait_recv()
        few = pl.ds(96 * n, size_of(n) // 4)
        v = [yv[slot, i, few, :].astype(F32) + yv[slot, 4 + i, few, :].astype(F32) * sign_c for i in range(4)]
        p0, p1, n0, n1 = v[0] + v[1], v[2] + v[3], v[0] - v[1], v[2] - v[3]
        scale = 0.25 if slot else 1.0
        for i, value in enumerate((p0 + p1, n0 + n1, p0 - p1, n0 - n1)):
            yo[slot, i, few, :] = (value * scale).astype(BF16)
        dst = dst_of[slot]
        over_back[slot, n] = [
            send(yo.at[slot, lax.rem(y + k, 4), few], dst.at[part_at(n, y)], at_y(k)) for k in (2, 1, 3)
        ]
        dst[part_at(n, y), :] = yo[slot, y, few, :]

    def had4(slot, n):
        for copy in over_back[slot, n]:
            copy.wait_recv()

    got_p, got_m = {}, {}

    def ag(k, n):
        rows = rows_of(n)
        if k == 1:
            had4(0, n)
            got_p[1, n] = send(h_buf.at[rows], fp.at[0, rows], at_z(1))
            got_m[1, n] = send(h_buf.at[rows], fm.at[0, rows], at_z(-1))
            return
        got_p[k - 1, n].wait_recv()
        if k < 4 or n in HALF_A:
            got_p[k, n] = send(fp.at[k - 2, rows], fp.at[k - 1, rows], at_z(1))
        got_m[k - 1, n].wait_recv()
        if k < 4 or n in HALF_B:
            got_m[k, n] = send(fm.at[k - 2, rows], fm.at[k - 1, rows], at_z(-1))

    og_all = og.reshape(4 * TOK, DG)
    og_near = []

    def og_on():
        for k, copies in zip((3, 1, 2), og_far):
            for copy in copies:
                copy.wait_recv()
            og_near.append(send(og.at[k, half], og.at[k, half], other))

    def grad_part(n):
        while og_near:
            og_near.pop().wait_recv()
            if not og_near:
                loads["og"].wait()
        for copy in w_two[n]:
            copy.wait_recv()
        unpack(n)
        rows = rows_of(n)
        part = lax.dot_general(
            wfull[rows, :], og_all[...], (((1,), (1,)), ((), ())), preferred_element_type=F32
        )
        for k in range(4):
            pk[k, rows, :] = part[:, k * TOK : (k + 1) * TOK]

    def sign_of(at):
        far = lax.div(lax.rem(pos + 8 + at, 8), 4)
        return jnp.where(far * zh == 1, -1.0, 1.0).astype(F32)

    sum_p, sum_m = {}, {}

    def send_sum(up, d, n):
        rows = rows_of(n)
        kept, got, out, way = (sum_p, rp, sp, 1) if up else (sum_m, rm, sm, -1)
        value = pk[way * d % 4, rows, :] * sign_of(way * d)
        if (d, n) in kept:
            kept[d, n].wait_recv()
            value = value + got[d, rows, :].astype(F32)
        out[d - 1, rows, :] = value.astype(BF16)
        kept[d - 1, n] = send(out.at[d - 1, rows], got.at[d - 1, rows], at_z(way))

    def rs(step, n):
        long_up = n in HALF_A
        for up in (long_up, not long_up):
            d = (4 if up == long_up else 3) - step
            if d >= 1:
                send_sum(up, d, n)

    def rs_end(n):
        rows = rows_of(n)
        sum_p[0, n].wait_recv()
        sum_m[0, n].wait_recv()
        value = pk[0, rows, :] * sign_of(0)
        value = value + rp[0, rows, :].astype(F32) + rm[0, rows, :].astype(F32)
        mix[1, rows, :] = value.astype(BF16)
        had2(1, n)

    def rotated(n):
        rows = rows_of(n)
        (got_p if n in HALF_A else got_m)[4, n].wait_recv()
        for k in range(4):
            mine = h_buf if k == 0 else fm.at[k - 1]
            far = fp.at[3 - k] if k else (fp if n in HALF_A else fm).at[3]
            value = mine[rows, :].astype(F32) * (sign_of(k) * 0.25)
            value = value + far[rows, :].astype(F32) * (sign_of(k + 4) * 0.25)
            rott[rows, pl.ds(k * TOK, TOK)] = value.astype(BF16)

    def weight_grad(n):
        rows, groups = rows_of(n), size_of(n) // 64
        part = jnp.dot(rott[rows, :], og_all[...], preferred_element_type=F32)
        part = part * wfull[rows, :].astype(F32)
        s3[n, 6:8, :] = jnp.zeros((2, DG), F32)
        s3[n, 0:groups, :] = jnp.sum(part.reshape(groups, 64, DG), axis=1)

    def s_lanes(j):
        xs = lax.rem(x + 4 + j, 4)
        return pl.ds(pl.multiple_of((lax.div(xs, 2) * 5 + lax.rem(xs, 2) * 2) * 128, 128), 384)

    ls_copies = []

    def ls_send():
        ls_copies.extend(send(s3.at[:, :, s_lanes(j)], lsb.at[j - 1], at_x(j)) for j in (1, 2, 3))

    def ls_end():
        for copy in ls_copies:
            copy.wait_recv()
        total = s3[:, :, s_lanes(0)]
        for j in range(3):
            total = total + lsb[j]
        total = total.reshape(32, 384)
        o_ls[...] = jnp.where(odd == 1, pltpu.roll(total, 320, 1), total)[:, :DROW]

    summed = []

    def last_part(n):
        had4(1, n)
        again = bool(summed)
        summed.append(n)

        def last_rows(i, _):
            rows = pl.ds(pl.multiple_of(i * 320, 16), 320)
            grad = jnp.dot(rot[rows, 384 * n : 384 * n + size_of(n)], g_buf[rows_of(n), :], preferred_element_type=F32)
            o_gh[rows, :] = o_gh[rows, :] + grad if again else grad
            return 0

        lax.fori_loop(0, 5, last_rows, 0)

    steps = dict(
        weights=weights, weights_on=weights_on, hidden=hidden, mixed=mixed, had3=had3, ag=ag, rs=rs,
        og_on=og_on, grad_part=grad_part, rs_end=rs_end, rotated=rotated, weight_grad=weight_grad,
        ls_send=ls_send, ls_end=ls_end, last_part=last_part,
    )
    for name, *at in ORDER:
        steps[name](*at)
    for copy in pending:
        copy.wait_send()


def finish(gh, g, u, ls, o_gg, o_gu, o_ls):
    grad, gate, up = gh[...], g[...].astype(F32), u[...].astype(F32)
    sig = 1.0 / (1.0 + jnp.exp(-gate))
    o_gg[...] = (grad * up * sig * (1.0 + gate * (1.0 - sig))).astype(BF16)
    o_gu[...] = (grad * gate * sig).astype(BF16)
    for n in range(4):
        groups = size_of(n) // 64
        o_ls[6 * n : 6 * n + groups, :] = ls[8 * n : 8 * n + groups, :]


def on_device(out_grad, gate_act, up_act, codes, zero_points, scales, rotation):
    vm = pl.BlockSpec(memory_space=pltpu.VMEM)
    hbm = pl.BlockSpec(memory_space=pl.ANY)
    gate_t, up_t = gate_act.T, up_act.T
    gh, ls = pl.pallas_call(
        kernel,
        out_shape=(
            jax.ShapeDtypeStruct((BLK, TOK), F32),
            jax.ShapeDtypeStruct((32, DROW), F32),
        ),
        in_specs=[hbm] * 7,
        out_specs=(vm, vm),
        scratch_shapes=[
            pltpu.VMEM((DROW, BLK), jnp.int32),
            pltpu.VMEM((BLK, BLK), BF16),
            pltpu.VMEM((BLK, TOK), BF16),
            pltpu.VMEM((BLK, TOK), BF16),
            pltpu.VMEM((BLK, DG), BF16),
            pltpu.VMEM((4, REST, 128), BF16),
            pltpu.VMEM((4, TOK, DG), BF16),
            pltpu.VMEM((TOK, BLK), BF16),
            pltpu.VMEM((BLK, TOK), BF16),
            pltpu.VMEM((2, BLK, TOK), BF16),
            pltpu.VMEM((2, 8, BLK // 4, TOK), BF16),
            pltpu.VMEM((2, 4, BLK // 4, TOK), BF16),
            pltpu.VMEM((BLK, TOK), BF16),
            pltpu.VMEM((4, BLK, TOK), BF16),
            pltpu.VMEM((4, BLK, TOK), BF16),
            pltpu.VMEM((BLK, 4 * TOK), BF16),
            pltpu.VMEM((4, BLK, TOK), F32),
            pltpu.VMEM((4, BLK, TOK), BF16),
            pltpu.VMEM((4, BLK, TOK), BF16),
            pltpu.VMEM((4, BLK, TOK), BF16),
            pltpu.VMEM((4, BLK, TOK), BF16),
            pltpu.VMEM((BLK, TOK), BF16),
            pltpu.VMEM((4, 8, DG), F32),
            pltpu.VMEM((3, 4, 8, 384), F32),
            pltpu.VMEM((25, DROW), jnp.int32),
            pltpu.VMEM((25, DROW), F32),
            pltpu.VMEM((32, 512), F32),
            pltpu.VMEM((32, 512), F32),
            pltpu.SemaphoreType.DMA((13,)),
            pltpu.SemaphoreType.DMA((N_COPY,)),
            pltpu.SemaphoreType.DMA((N_COPY,)),
        ],
        name="whole",
        compiler_params=pltpu.CompilerParams(
            collective_id=0, has_side_effects=True, vmem_limit_bytes=56 << 20
        ),
    )(out_grad, gate_t, up_t, codes, zero_points.T, scales.T, rotation)
    part = pl.BlockSpec((BLK // 2, TOK), lambda i: (i, 0))
    gg, gu, ls = pl.pallas_call(
        finish,
        grid=(2,),
        out_shape=(
            jax.ShapeDtypeStruct((BLK, TOK), BF16),
            jax.ShapeDtypeStruct((BLK, TOK), BF16),
            jax.ShapeDtypeStruct((25, DROW), F32),
        ),
        in_specs=[part, part, part, pl.BlockSpec((32, DROW), lambda i: (0, 0))],
        out_specs=(part, part, pl.BlockSpec((25, DROW), lambda i: (0, 0))),
        name="finish",
    )(gh, gate_t, up_t, ls)
    return gg.T, gu.T, ls.T


def solution(mesh):
    return jax.shard_map(
        on_device,
        mesh=mesh,
        in_specs=(
            P("dp", None),
            P("dp", "tensor"),
            P("dp", "tensor"),
            P("dp", "tensor"),
            P("dp", "tensor"),
            P("dp", "tensor"),
            P(),
        ),
        out_specs=(P("dp", "tensor"), P("dp", "tensor"), P("dp", "tensor")),
        check_vma=False,
    )
```

```python
import jax
import jax.numpy as jnp
from jax import lax
from jax.experimental import pallas as pl
from jax.experimental.pallas import tpu as pltpu
from jax.sharding import PartitionSpec as P

MESH = pl.DeviceIdType.MESH
F32 = jnp.float32
BF16 = jnp.bfloat16
TOK = 128
BLK = 1600
DROW = 320
DG = 1280
REST = 832
HALF_A, HALF_B = (0, 2), (1, 3)
N_COPY = 178


ORDER = (
    ("hidden",), ("mixed", 0), ("weights", 0), ("mixed", 1), ("had3", 0, 0), ("mixed", 2), ("weights", 1),
    ("had3", 0, 1), ("mixed", 3), ("ag", 1, 0), ("weights_on", 0), ("had3", 0, 2), ("ag", 1, 1), ("og_on",),
    ("weights", 2), ("ag", 2, 0), ("had3", 0, 3), ("weights", 3), ("ag", 1, 2), ("grad_part", 0), ("rs", 0, 0),
    ("ag", 3, 0), ("ag", 2, 2), ("rs", 1, 0), ("ag", 2, 1), ("ag", 1, 3), ("weights_on", 1), ("weights_on", 3),
    ("rs", 2, 0), ("grad_part", 1), ("rs", 0, 1), ("ag", 3, 1), ("weights_on", 2), ("grad_part", 3), ("rs", 0, 3),
    ("rs", 1, 1), ("grad_part", 2), ("rs", 0, 2), ("rs", 1, 3), ("rs", 2, 1), ("rs", 1, 2), ("ag", 4, 1),
    ("rs", 3, 0), ("rs", 2, 3), ("ag", 4, 0), ("rs", 2, 2), ("rs", 3, 1), ("rs_end", 0), ("ag", 2, 3), ("rs", 3, 3),
    ("ag", 3, 2), ("rotated", 1), ("rotated", 0), ("rs_end", 1), ("rs", 3, 2), ("had3", 1, 0), ("ag", 3, 3),
    ("weight_grad", 0), ("weight_grad", 1), ("rs_end", 3), ("rs_end", 2), ("ag", 4, 2), ("had3", 1, 1), ("ag", 4, 3),
    ("last_part", 0), ("had3", 1, 3), ("rotated", 2), ("weight_grad", 2), ("had3", 1, 2), ("rotated", 3),
    ("weight_grad", 3), ("ls_send",), ("last_part", 1), ("last_part", 3), ("last_part", 2), ("ls_end",),
)

def rows_of(n):
    return pl.ds(384 * n, size_of(n))


def size_of(n):
    return 384 if n < 3 else 448


def kernel(
    og_in, g_in, u_in, codes_in, zp_in, sc_in, rot_in,
    o_gh, o_ls,
    codes, rot, g_v, u_v, wfull, wrecv, og, hid, m_buf, mix, yv, yo, h_buf, fp, fm, rott, pk,
    sp, sm, rp, rm, g_buf, s3, lsb, z_v, s_v, zps, scs, lsem, ssem, rsem,
):
    dp = lax.axis_index("dp")
    tn = lax.axis_index("tensor")
    x, zl = lax.rem(dp, 4), lax.div(dp, 4)
    y, zh, c = lax.div(tn, 4), lax.rem(lax.div(tn, 2), 2), lax.rem(tn, 2)
    pos = zh * 4 + zl
    odd = lax.rem(x, 2)

    def at_x(k):
        return (zl * 4 + lax.rem(x + 4 + k, 4), tn)

    def at_y(k):
        return (dp, lax.rem(y + 4 + k, 4) * 4 + zh * 2 + c)

    def across(k):
        return (dp, lax.rem(y + 4 + k, 4) * 4 + zh * 2 + 1 - c)

    def at_z(k):
        to = lax.rem(pos + 8 + k, 8)
        return (lax.rem(to, 4) * 4 + x, y * 4 + lax.div(to, 4) * 2 + c)

    other = across(0)

    def og_cols(k):
        return pl.ds(pl.multiple_of(lax.rem(zl + 4 + k, 4) * DG, 128), DG)

    moves = {"gate": (g_in, g_v), "up": (u_in, u_v), "zp": (zp_in, z_v), "sc": (sc_in, s_v)}
    for n in range(4):
        cols = rows_of(n)
        moves["rot", n] = (rot_in.at[:, cols], rot.at[:, cols])
        moves["codes", n] = (codes_in.at[:, cols], codes.at[:, cols])
    moves["og"] = (og_in.at[:, og_cols(0)], og.at[0])
    loads = {
        name: pltpu.make_async_copy(src, dst, lsem.at[i])
        for i, (name, (src, dst)) in enumerate(moves.items())
    }
    def load(*names):
        for name in names:
            loads[name].start()

    load("gate", "up", ("rot", 0))

    count = [0]
    pending = []

    def send(src, dst, device):
        i = count[0]
        count[0] += 1
        copy = pltpu.make_async_remote_copy(
            src_ref=src, dst_ref=dst, send_sem=ssem.at[i], recv_sem=rsem.at[i],
            device_id=device, device_id_type=MESH,
        )
        copy.start()
        pending.append(copy)
        return copy

    barrier = pltpu.get_barrier_semaphore()
    peers = [at_x(1), at_x(2), at_x(3), at_y(1), at_y(2), at_y(3)]
    peers += [at_z(1), at_z(-1), at_z(2), at_z(-2), other, across(1), across(2), across(3)]
    for peer in peers:
        pl.semaphore_signal(barrier, inc=1, device_id=peer, device_id_type=MESH)
    pl.semaphore_wait(barrier, len(peers))

    half = pl.ds(pl.multiple_of(c * 64, 64), 64)
    first, second = (pl.ds(pl.multiple_of(c * 64 + i * 32, 32), 32) for i in (0, 1))
    og_far = []

    def og_start():
        og_far.append((send(og_in.at[half, og_cols(1)], og.at[3, half], at_z(1)),))
        og_far.append((send(og_in.at[half, og_cols(-1)], og.at[1, half], at_z(-1)),))
        og_far.append((
            send(og_in.at[first, og_cols(2)], og.at[2, first], at_z(2)),
            send(og_in.at[second, og_cols(2)], og.at[2, second], at_z(-2)),
        ))

    def lanes_of(j):
        xs = lax.rem(x + 4 + j, 4)
        return pl.ds(pl.multiple_of((lax.div(xs, 2) * 5 + lax.rem(xs, 2) * 3) * 128, 128), 256)

    def main_part(j, n, part, parts):
        size = size_of(n) // parts
        return wfull.at[pl.ds(384 * n + part * size, size), lanes_of(j)]

    def rest_part(j, n, part, parts):
        size = (192 if n < 3 else 256) // parts
        return wrecv.at[lax.rem(x + 4 + j, 4), pl.ds(192 * n + part * size, size)]

    def place(src, dst):
        dst[0:25, 0:DROW] = src[...].astype(F32)
        value = dst[:, 0:384]
        main = jnp.where(odd == 1, pltpu.roll(value, 320, 1), value)[:, :256]
        rest = jnp.where(odd == 1, value[:, :128], value[:, 256:])
        dst[:, 0:256] = main
        dst[:, 256:384] = rest
        dst[:, 384:512] = pltpu.roll(rest, 64, 1)

    def rest_of(src, g):
        here, after = src[pl.ds(g, 1), :], src[pl.ds(g + 1, 1), :]
        left, right = jnp.where(odd == 1, after, here), jnp.where(odd == 1, here, after)
        return jnp.where(low[:1], left[:, 256:384], right[:, 384:512])

    low = lax.broadcasted_iota(jnp.int32, (64, 128), 1) < 64
    main_rows = pl.ds(pl.multiple_of(odd * 64, 64), 256)
    rest_rows = pl.ds(pl.multiple_of(256 - odd * 256, 64), 64)

    def weight_tile(i, width):
        at = pl.ds(i * 128, width) if isinstance(i, int) else pl.ds(pl.multiple_of(i * 128, 128), width)
        main = codes[main_rows, at].astype(F32).T
        rest = codes[rest_rows, at].astype(F32)
        if width == 128:
            turned = pltpu.roll(rest, 64, 1)
            stack = jnp.where(odd == 1, jnp.concatenate([turned, rest]), jnp.concatenate([rest, turned]))
            packed = stack.T[:64]
        else:
            packed = jnp.concatenate([rest, rest]).T
        for k in range(width // 64):
            g = 2 * i + k
            value = (main[64 * k : 64 * k + 64] - zps[pl.ds(g, 1), 0:256]) * scs[pl.ds(g, 1), 0:256]
            wfull[pl.ds(i * 128 + 64 * k if isinstance(i, int) else pl.multiple_of(i * 128 + 64 * k, 64), 64), lanes_of(0)] = value.astype(BF16)
        if width == 128:
            zp, sc = rest_of(zps, 2 * i), rest_of(scs, 2 * i)
        else:
            zp, sc = (jnp.where(low[:1], a[24:25, 256:384], a[24:25, 384:512]) for a in (zps, scs))
        wrecv[x, pl.ds(i * 64 if isinstance(i, int) else pl.multiple_of(i * 64, 64), 64), :] = ((packed - zp) * sc).astype(BF16)

    w_plus, w_minus, w_two = {}, {}, {}

    def weights(n):
        def step(i, _):
            weight_tile(3 * n + i, 128)
            return 0

        if n == 0:
            loads["zp"].wait()
            loads["sc"].wait()
            place(z_v, zps)
            place(s_v, scs)
        loads["codes", n].wait()
        lax.fori_loop(0, 3, step, 0)
        if n == 3:
            weight_tile(12, 64)
        for kept, k in ((w_plus, 1), (w_minus, -1)):
            kept[n] = [send(part(0, n, 0, 1), part(0, n, 0, 1), at_x(k)) for part in (main_part, rest_part)]

    def weights_on(n):
        for copy in w_plus[n]:
            copy.wait_recv()
        w_two[n] = [send(part(-1, n, 0, 2), part(-1, n, 0, 2), at_x(1)) for part in (main_part, rest_part)]
        for copy in w_minus[n]:
            copy.wait_recv()
        w_two[n] += [send(part(1, n, 1, 2), part(1, n, 1, 2), at_x(-1)) for part in (main_part, rest_part)]

    def unpack(n):
        for i in range(3 * n, 3 * n + (3 if n < 3 else 4)):
            for pair in range(2):
                even = wrecv[2 * pair, pl.ds(64 * i, 64), :].astype(F32)
                next_ = wrecv[2 * pair + 1, pl.ds(64 * i, 64), :].astype(F32)
                lanes = pl.ds((pair * 5 + 2) * 128, 128)
                wfull[pl.ds(128 * i, 64), lanes] = jnp.where(low, even, next_).astype(BF16)
                if i < 12:
                    turned = pltpu.roll(jnp.where(low, next_, even), 64, 1)
                    wfull[pl.ds(128 * i + 64, 64), lanes] = turned.astype(BF16)

    def hidden_rows(i, _):
        rows = pl.ds(pl.multiple_of(i * 320, 16), 320)
        gate = g_v[rows, :].astype(F32)
        up = u_v[rows, :].astype(F32)
        m_buf[rows, :] = (gate * (1.0 / (1.0 + jnp.exp(-gate))) * up).astype(BF16)
        return 0

    def hidden():
        loads["gate"].wait()
        loads["up"].wait()
        lax.fori_loop(0, 5, hidden_rows, 0)
        hid[...] = m_buf[...].astype(F32).T.astype(BF16)
        load(("codes", 0), "zp", "sc", ("rot", 1))

    def mixed(n):
        loads["rot", n].wait()
        part = jnp.dot(hid[...], rot[:, 384 * n : 384 * n + size_of(n)], preferred_element_type=F32)
        mix[0, rows_of(n), :] = part.T.astype(BF16)
        had2(0, n)
        if n == 0:
            load(("rot", 2), ("rot", 3))
            og_start()
        elif n == 1:
            load(("codes", 1), ("codes", 2), ("codes", 3), "og")

    sign_c = jnp.where(c == 1, -1.0, 1.0).astype(F32)
    over_y, over_back = {}, {}
    dst_of = (h_buf, g_buf)

    def part_at(n, i):
        size = size_of(n) // 4
        return pl.ds(pl.multiple_of(384 * n + i * size, 16), size)

    def had2(slot, n):
        src, few = mix.at[slot], pl.ds(96 * n, size_of(n) // 4)
        over_y[slot, n] = [
            send(src.at[part_at(n, lax.rem(y + k, 4))], yv.at[slot, 4 * c + y, few], to(k))
            for to, k in ((across, 2), (at_y, 2), (across, 1), (at_y, 1), (across, 3), (at_y, 3), (across, 0))
        ]
        yv[slot, 4 * c + y, few, :] = src[part_at(n, y), :]

    def had3(slot, n):
        for copy in over_y[slot, n]:
            copy.wait_recv()
        few = pl.ds(96 * n, size_of(n) // 4)
        v = [yv[slot, i, few, :].astype(F32) + yv[slot, 4 + i, few, :].astype(F32) * sign_c for i in range(4)]
        p0, p1, n0, n1 = v[0] + v[1], v[2] + v[3], v[0] - v[1], v[2] - v[3]
        scale = 0.25 if slot else 1.0
        for i, value in enumerate((p0 + p1, n0 + n1, p0 - p1, n0 - n1)):
            yo[slot, i, few, :] = (value * scale).astype(BF16)
        dst = dst_of[slot]
        over_back[slot, n] = [
            send(yo.at[slot, lax.rem(y + k, 4), few], dst.at[part_at(n, y)], at_y(k)) for k in (2, 1, 3)
        ]
        dst[part_at(n, y), :] = yo[slot, y, few, :]

    def had4(slot, n):
        for copy in over_back[slot, n]:
            copy.wait_recv()

    got_p, got_m = {}, {}

    def ag(k, n):
        rows = rows_of(n)
        if k == 1:
            had4(0, n)
            got_p[1, n] = send(h_buf.at[rows], fp.at[0, rows], at_z(1))
            got_m[1, n] = send(h_buf.at[rows], fm.at[0, rows], at_z(-1))
            return
        got_p[k - 1, n].wait_recv()
        if k < 4 or n in HALF_A:
            got_p[k, n] = send(fp.at[k - 2, rows], fp.at[k - 1, rows], at_z(1))
        got_m[k - 1, n].wait_recv()
        if k < 4 or n in HALF_B:
            got_m[k, n] = send(fm.at[k - 2, rows], fm.at[k - 1, rows], at_z(-1))

    og_all = og.reshape(4 * TOK, DG)
    og_near = []

    def og_on():
        for k, copies in zip((3, 1, 2), og_far):
            for copy in copies:
                copy.wait_recv()
            og_near.append(send(og.at[k, half], og.at[k, half], other))

    def grad_part(n):
        while og_near:
            og_near.pop().wait_recv()
            if not og_near:
                loads["og"].wait()
        for copy in w_two[n]:
            copy.wait_recv()
        unpack(n)
        rows = rows_of(n)
        part = lax.dot_general(
            wfull[rows, :], og_all[...], (((1,), (1,)), ((), ())), preferred_element_type=F32
        )
        for k in range(4):
            pk[k, rows, :] = part[:, k * TOK : (k + 1) * TOK]

    def sign_of(at):
        far = lax.div(lax.rem(pos + 8 + at, 8), 4)
        return jnp.where(far * zh == 1, -1.0, 1.0).astype(F32)

    sum_p, sum_m = {}, {}

    def send_sum(up, d, n):
        rows = rows_of(n)
        kept, got, out, way = (sum_p, rp, sp, 1) if up else (sum_m, rm, sm, -1)
        value = pk[way * d % 4, rows, :] * sign_of(way * d)
        if (d, n) in kept:
            kept[d, n].wait_recv()
            value = value + got[d, rows, :].astype(F32)
        out[d - 1, rows, :] = value.astype(BF16)
        kept[d - 1, n] = send(out.at[d - 1, rows], got.at[d - 1, rows], at_z(way))

    def rs(step, n):
        long_up = n in HALF_A
        for up in (long_up, not long_up):
            d = (4 if up == long_up else 3) - step
            if d >= 1:
                send_sum(up, d, n)

    def rs_end(n):
        rows = rows_of(n)
        sum_p[0, n].wait_recv()
        sum_m[0, n].wait_recv()
        value = pk[0, rows, :] * sign_of(0)
        value = value + rp[0, rows, :].astype(F32) + rm[0, rows, :].astype(F32)
        mix[1, rows, :] = value.astype(BF16)
        had2(1, n)

    def rotated(n):
        rows = rows_of(n)
        (got_p if n in HALF_A else got_m)[4, n].wait_recv()
        for k in range(4):
            mine = h_buf if k == 0 else fm.at[k - 1]
            far = fp.at[3 - k] if k else (fp if n in HALF_A else fm).at[3]
            value = mine[rows, :].astype(F32) * (sign_of(k) * 0.25)
            value = value + far[rows, :].astype(F32) * (sign_of(k + 4) * 0.25)
            rott[rows, pl.ds(k * TOK, TOK)] = value.astype(BF16)

    def weight_grad(n):
        rows, groups = rows_of(n), size_of(n) // 64
        part = jnp.dot(rott[rows, :], og_all[...], preferred_element_type=F32)
        part = part * wfull[rows, :].astype(F32)
        s3[n, 6:8, :] = jnp.zeros((2, DG), F32)
        s3[n, 0:groups, :] = jnp.sum(part.reshape(groups, 64, DG), axis=1)

    def s_lanes(j):
        xs = lax.rem(x + 4 + j, 4)
        return pl.ds(pl.multiple_of((lax.div(xs, 2) * 5 + lax.rem(xs, 2) * 2) * 128, 128), 384)

    ls_copies = []

    def ls_send():
        ls_copies.extend(send(s3.at[:, :, s_lanes(j)], lsb.at[j - 1], at_x(j)) for j in (1, 2, 3))

    def ls_end():
        for copy in ls_copies:
            copy.wait_recv()
        total = s3[:, :, s_lanes(0)]
        for j in range(3):
            total = total + lsb[j]
        total = total.reshape(32, 384)
        o_ls[...] = jnp.where(odd == 1, pltpu.roll(total, 320, 1), total)[:, :DROW]

    summed = []

    def last_part(n):
        had4(1, n)
        again = bool(summed)
        summed.append(n)

        def last_rows(i, _):
            rows = pl.ds(pl.multiple_of(i * 320, 16), 320)
            grad = jnp.dot(rot[rows, 384 * n : 384 * n + size_of(n)], g_buf[rows_of(n), :], preferred_element_type=F32)
            o_gh[rows, :] = o_gh[rows, :] + grad if again else grad
            return 0

        lax.fori_loop(0, 5, last_rows, 0)

    steps = dict(
        weights=weights, weights_on=weights_on, hidden=hidden, mixed=mixed, had3=had3, ag=ag, rs=rs,
        og_on=og_on, grad_part=grad_part, rs_end=rs_end, rotated=rotated, weight_grad=weight_grad,
        ls_send=ls_send, ls_end=ls_end, last_part=last_part,
    )
    for name, *at in ORDER:
        steps[name](*at)
    for copy in pending:
        copy.wait_send()


def finish(gh, g, u, ls, o_gg, o_gu, o_ls):
    grad, gate, up = gh[...], g[...].astype(F32), u[...].astype(F32)
    sig = 1.0 / (1.0 + jnp.exp(-gate))
    o_gg[...] = (grad * up * sig * (1.0 + gate * (1.0 - sig))).astype(BF16)
    o_gu[...] = (grad * gate * sig).astype(BF16)
    for n in range(4):
        groups = size_of(n) // 64
        o_ls[6 * n : 6 * n + groups, :] = ls[8 * n : 8 * n + groups, :]


def on_device(out_grad, gate_act, up_act, codes, zero_points, scales, rotation):
    vm = pl.BlockSpec(memory_space=pltpu.VMEM)
    hbm = pl.BlockSpec(memory_space=pl.ANY)
    gate_t, up_t = gate_act.T, up_act.T
    gh, ls = pl.pallas_call(
        kernel,
        out_shape=(
            jax.ShapeDtypeStruct((BLK, TOK), F32),
            jax.ShapeDtypeStruct((32, DROW), F32),
        ),
        in_specs=[hbm] * 7,
        out_specs=(vm, vm),
        scratch_shapes=[
            pltpu.VMEM((DROW, BLK), jnp.int32),
            pltpu.VMEM((BLK, BLK), BF16),
            pltpu.VMEM((BLK, TOK), BF16),
            pltpu.VMEM((BLK, TOK), BF16),
            pltpu.VMEM((BLK, DG), BF16),
            pltpu.VMEM((4, REST, 128), BF16),
            pltpu.VMEM((4, TOK, DG), BF16),
            pltpu.VMEM((TOK, BLK), BF16),
            pltpu.VMEM((BLK, TOK), BF16),
            pltpu.VMEM((2, BLK, TOK), BF16),
            pltpu.VMEM((2, 8, BLK // 4, TOK), BF16),
            pltpu.VMEM((2, 4, BLK // 4, TOK), BF16),
            pltpu.VMEM((BLK, TOK), BF16),
            pltpu.VMEM((4, BLK, TOK), BF16),
            pltpu.VMEM((4, BLK, TOK), BF16),
            pltpu.VMEM((BLK, 4 * TOK), BF16),
            pltpu.VMEM((4, BLK, TOK), F32),
            pltpu.VMEM((4, BLK, TOK), BF16),
            pltpu.VMEM((4, BLK, TOK), BF16),
            pltpu.VMEM((4, BLK, TOK), BF16),
            pltpu.VMEM((4, BLK, TOK), BF16),
            pltpu.VMEM((BLK, TOK), BF16),
            pltpu.VMEM((4, 8, DG), F32),
            pltpu.VMEM((3, 4, 8, 384), F32),
            pltpu.VMEM((25, DROW), jnp.int32),
            pltpu.VMEM((25, DROW), F32),
            pltpu.VMEM((32, 512), F32),
            pltpu.VMEM((32, 512), F32),
            pltpu.SemaphoreType.DMA((13,)),
            pltpu.SemaphoreType.DMA((N_COPY,)),
            pltpu.SemaphoreType.DMA((N_COPY,)),
        ],
        name="whole",
        compiler_params=pltpu.CompilerParams(
            collective_id=0, has_side_effects=True, vmem_limit_bytes=56 << 20
        ),
    )(out_grad, gate_t, up_t, codes, zero_points.T, scales.T, rotation)
    part = pl.BlockSpec((BLK // 2, TOK), lambda i: (i, 0))
    gg, gu, ls = pl.pallas_call(
        finish,
        grid=(2,),
        out_shape=(
            jax.ShapeDtypeStruct((BLK, TOK), BF16),
            jax.ShapeDtypeStruct((BLK, TOK), BF16),
            jax.ShapeDtypeStruct((25, DROW), F32),
        ),
        in_specs=[part, part, part, pl.BlockSpec((32, DROW), lambda i: (0, 0))],
        out_specs=(part, part, pl.BlockSpec((25, DROW), lambda i: (0, 0))),
        name="finish",
    )(gh, gate_t, up_t, ls)
    return gg.T, gu.T, ls.T


def solution(mesh):
    return jax.shard_map(
        on_device,
        mesh=mesh,
        in_specs=(
            P("dp", None),
            P("dp", "tensor"),
            P("dp", "tensor"),
            P("dp", "tensor"),
            P("dp", "tensor"),
            P("dp", "tensor"),
            P(),
        ),
        out_specs=(P("dp", "tensor"), P("dp", "tensor"), P("dp", "tensor")),
        check_vma=False,
    )
```
